32 devices in a mesh: grp: 8 (over z, core), exp: 4 (over y, x).
Axes of the slice: x: 2, y: 2, z: 4, core: 2. Of those that a mesh axis runs over, the one named last changes fastest.
Arguments:
- sky: float32 [32, 6, 8, 512], P(('grp', 'exp')), may hold values from -6 to 6
- observed: bfloat16 [128, 6, 8, 512], P(('grp', 'exp')), may hold values from -6 to 6
- intersections: int32 [128, 4], P(('grp', 'exp')), may hold values from 0 to 7
- resample_index: int32 [128, 4], P(('grp', 'exp')), may hold values from 0 to 7
- psf_index: int32 [128], P(('grp', 'exp')), may hold values from 0 to 15
- resample_table: bfloat16 [8, 512, 512], replicated, may hold values from -0.25 to 0.25
- psf_weights: float32 [16, 8], replicated, may hold values from -5 to 5
- psf_basis: float32 [8, 41], replicated, may hold values from -0.3125 to 0.3125
Outputs:
- sky_out: float32 [32, 6, 8, 512], P(('grp', 'exp'))
- residual: float32 [128, 6, 8, 512], P(('grp', 'exp'))
The draws below stay inside these ranges and needn't reach their ends.
Inputs may be any that keep to these rules, and one draw needn't show every extreme that they name: `intersections`: with G = 4: an entry v below G names tile v of the exposure's own group; an entry v of G or more names tile v - G of the next group along grp, cyclically.
All inputs are finite; a program needn't handle non-finite values.
Results may differ from the reference program's by a relative error of at most 0.019.
Values may be sent and summed in bfloat16 or wider, within the bound.
A program may use at most 128 MiB of HBM per device.

```python
import jax
import jax.numpy as jnp
from jax import lax

BANDS = 6
WIDTH = 512
ROWS = 8
TAPS = 41
COMP = 8
INTERSECTIONS = 4
NRES = 8
NPSF = 16
ITERS = 2
TILES_DEV = 1
EXP_DEV = 4
TILES = 32
EXPOSURES = 128
N_GRP = 8
N_EXP = 4


def set_ends(entries, rng, least, largest):
    spot = [jax.random.randint(jax.random.fold_in(rng, axis), (), 0, length) for axis, length in enumerate(entries.shape)]
    main_axis = entries.shape.index(max(entries.shape))
    neighbour = spot[:main_axis] + [(spot[main_axis] + 1) % entries.shape[main_axis]] + spot[main_axis + 1:]
    return entries.at[tuple(spot)].set(least).at[tuple(neighbour)].set(largest)


def shard_levels(key, extent, split, least, top_value):
    gain = 1.0
    for dim, blocks in split:
        heights = jax.random.uniform(jax.random.fold_in(jax.random.fold_in(key, 6), dim), (blocks,), jnp.float32, least / len(split), top_value / len(split))
        gain = gain * jnp.repeat(jnp.exp(heights), extent[dim] // blocks).reshape((-1,) + (1,) * (len(extent) - 1 - dim))
    return gain


def noise(own_key, shape, width, reach, shards=(), kind=jnp.bfloat16):
    entries = width * jax.random.normal(own_key, shape, jnp.float32)
    if shards:
        entries = entries * shard_levels(own_key, shape, shards, -0.22, 0.18)
    return jnp.clip(entries, -reach, reach).astype(kind)


def setup_inputs(seed: int = 0) -> dict:
    key_of = jax.random.split(jax.random.key(seed), 9)
    return {
        "sky": noise(key_of[0], (TILES, BANDS, ROWS, WIDTH), 1.0, 6.0, ((0, 32),), jnp.float32),
        "observed": noise(key_of[1], (EXPOSURES, BANDS, ROWS, WIDTH), 1.0, 6.0, ((0, 32),)),
        "intersections": set_ends(jax.random.randint(key_of[2], (EXPOSURES, INTERSECTIONS), 0, 2 * TILES_DEV * N_EXP), jax.random.fold_in(key_of[2], 1), 0, (2 * TILES_DEV * N_EXP) - 1).astype(jnp.int32),
        "resample_index": set_ends(jax.random.randint(key_of[3], (EXPOSURES, INTERSECTIONS), 0, NRES), jax.random.fold_in(key_of[3], 1), 0, NRES - 1).astype(jnp.int32),
        "psf_index": set_ends(jax.random.randint(key_of[4], (EXPOSURES,), 0, NPSF), jax.random.fold_in(key_of[4], 1), 0, NPSF - 1).astype(jnp.int32),
        "resample_table": noise(key_of[5], (NRES, WIDTH, WIDTH), WIDTH ** -0.5, 0.25),
        "psf_weights": noise(key_of[6], (NPSF, COMP), 1.0, 5.0, (), jnp.float32),
        "psf_basis": noise(key_of[7], (COMP, TAPS), (COMP * TAPS) ** -0.5, 0.3125, (), jnp.float32),
    }


def conv_matrix(kern):
    idx = jnp.arange(WIDTH, dtype=jnp.int32)
    diff = idx[:, None] - idx[None, :] + (TAPS - 1) // 2
    valid = (diff >= 0) & (diff < TAPS)
    values = jnp.take(kern, jnp.clip(diff, 0, TAPS - 1).astype(jnp.int32), axis=0)
    return jnp.where(valid, values, jnp.float32(0.0)).astype(jnp.bfloat16)


def reference(sky, observed, intersections, resample_index, psf_index, resample_table, psf_weights, psf_basis):
    group_tiles = TILES_DEV * N_EXP
    group_exp = EXP_DEV * N_EXP
    groups = jnp.arange(EXPOSURES, dtype=jnp.int32) // group_exp
    tile_id = (((groups[:, None] + intersections // group_tiles) % N_GRP) * group_tiles + intersections % group_tiles).astype(jnp.int32)
    kernels = jnp.sum(psf_weights[psf_index][:, :, None] * psf_basis[None, :, :], axis=1)
    flat = BANDS * ROWS
    sky_out = sky
    residual = jnp.zeros(observed.shape, jnp.float32)
    for step in range(ITERS):
        sky_half = sky_out.astype(jnp.bfloat16)

        def one(grads, item):
            ids, res_ids, kern, obs = item
            pre = jnp.zeros((flat, WIDTH), jnp.float32)
            for k in range(INTERSECTIONS):
                tile = sky_half[ids[k]].reshape(flat, WIDTH)
                pre = pre + jnp.dot(tile, resample_table[res_ids[k]], preferred_element_type=jnp.float32)
            conv = conv_matrix(kern)
            model = jnp.dot(pre.astype(jnp.bfloat16), conv, preferred_element_type=jnp.float32)
            resid = obs.reshape(flat, WIDTH).astype(jnp.float32) - model
            back = jnp.dot(resid.astype(jnp.bfloat16), conv.T, preferred_element_type=jnp.float32).astype(jnp.bfloat16)
            for k in range(INTERSECTIONS):
                part = jnp.dot(back, resample_table[res_ids[k]].T, preferred_element_type=jnp.float32)
                grads = grads.at[ids[k]].add(part.reshape(BANDS, ROWS, WIDTH))
            return grads, resid.reshape(BANDS, ROWS, WIDTH)

        grads, residual = lax.scan(one, jnp.zeros(sky.shape, jnp.float32), (tile_id, resample_index, kernels, observed))
        sky_out = sky_out + 0.05 * grads
    return sky_out, residual
```

```python
import functools

import jax
import jax.numpy as jnp
from jax import lax
from jax.experimental import pallas as pl
from jax.experimental.pallas import tpu as pltpu
from jax.sharding import PartitionSpec as P

ITERS = 2
STEP = 0.05
LANES = 128
MESH = pl.DeviceIdType.MESH
NN = (((1,), (0,)), ((), ()))
NT = (((1,), (1,)), ((), ()))


def dot(a, b, dims):
    return lax.dot_general(a, b, dims, preferred_element_type=jnp.float32)


def build_conv(psf_smem, weights_smem, basis_ref, taps_buf, conv_t):
    count, width, _ = conv_t.shape
    comp, taps = basis_ref.shape
    half = (taps - 1) // 2
    taps_buf[...] = jnp.zeros_like(taps_buf)
    taps_buf[:, : taps - half] = basis_ref[:, half:]
    taps_buf[:, 2 * LANES - half :] = basis_ref[:, :half]
    rows = lax.broadcasted_iota(jnp.int32, (LANES, LANES), 0)
    cols = lax.broadcasted_iota(jnp.int32, (LANES, LANES), 1)
    blank = jnp.zeros((LANES, LANES), jnp.bfloat16)
    blocks = width // LANES
    for e in range(count):
        kern = jnp.zeros((1, 2 * LANES), jnp.float32)
        for c in range(comp):
            kern = kern + weights_smem[psf_smem[e], c] * taps_buf[c : c + 1, :]
        wide = jnp.broadcast_to(kern, (LANES, 2 * LANES))
        rolled = pltpu.roll(wide, 0, 1, stride=1, stride_axis=0)
        edge = rolled[:, LANES:]
        diagonal = rolled[:, :LANES].astype(jnp.bfloat16)
        right = jnp.where(cols < rows, edge, 0.0).astype(jnp.bfloat16)
        left = jnp.where(cols > rows, edge, 0.0).astype(jnp.bfloat16)
        for i in range(blocks):
            for j in range(blocks):
                block = {0: diagonal, 1: right, -1: left}.get(j - i, blank)
                conv_t[e, i * LANES : (i + 1) * LANES, j * LANES : (j + 1) * LANES] = block


def kernel(
    n_grp, n_exp, tile_smem, res_smem, psf_smem, weights_smem, basis_ref, sky_ref, obs_ref, table_hbm,
    sky_out, resid_out,
    table, window, outbox, inbox, parts, conv_t, taps_buf,
    table_sem, fwd_send, fwd_recv, bwd_send, bwd_recv,
):
    g = lax.axis_index("grp")
    x = lax.axis_index("exp")
    before = lax.rem(g + n_grp - 1, n_grp)
    after = lax.rem(g + 1, n_grp)
    count, picks = tile_smem.shape

    load = pltpu.make_async_copy(table_hbm, table, table_sem)
    load.start()
    window[0, x] = sky_ref[...].astype(jnp.bfloat16)
    sky_out[...] = sky_ref[...]

    barrier = pltpu.get_barrier_semaphore()
    for j in range(n_exp):
        peer = lax.rem(x + j, n_exp)
        for group in (before, g, after):
            if j or group is not g:
                pl.semaphore_signal(barrier, inc=1, device_id=(group, peer), device_id_type=MESH)
    pl.semaphore_wait(barrier, 3 * n_exp - 1)

    def send(src, dst, send_sem, recv_sem, where):
        copy = pltpu.make_async_remote_copy(
            src_ref=src, dst_ref=dst, send_sem=send_sem, recv_sem=recv_sem, device_id=where, device_id_type=MESH
        )
        copy.start()
        return copy

    def spread(step):
        copies = []
        for j in range(n_exp):
            peer = lax.rem(x + j, n_exp)
            copies.append(send(
                window.at[step, x], window.at[step, n_exp + x], fwd_send.at[step, n_exp + j],
                fwd_recv.at[step, n_exp + x], (before, peer),
            ))
            if j:
                copies.append(send(
                    window.at[step, x], window.at[step, x], fwd_send.at[step, j], fwd_recv.at[step, x], (g, peer)
                ))
        return copies

    def arrive(buf, sem, step, slot):
        pltpu.make_async_copy(buf.at[step, slot], buf.at[step, slot], sem.at[step, slot]).wait()

    pending = spread(0)
    build_conv(psf_smem, weights_smem, basis_ref, taps_buf, conv_t)
    load.wait()

    for step in range(ITERS):
        for j in range(1, n_exp):
            arrive(window, fwd_recv, step, lax.rem(x + j, n_exp))
        for j in range(n_exp):
            arrive(window, fwd_recv, step, n_exp + j)

        for e in range(count):
            pre = dot(window[step, tile_smem[e, 0]], table[res_smem[e, 0]], NN)
            for k in range(1, picks):
                pre = pre + dot(window[step, tile_smem[e, k]], table[res_smem[e, k]], NN)
            model = dot(pre.astype(jnp.bfloat16), conv_t[e], NT)
            residual = obs_ref[e].astype(jnp.float32) - model
            if step == ITERS - 1:
                resid_out[e] = residual
            back = dot(residual.astype(jnp.bfloat16), conv_t[e], NN).astype(jnp.bfloat16)
            for k in range(picks):
                parts[e, k] = dot(back, table[res_smem[e, k]], NT)

        def gather(tile):
            total = jnp.zeros(sky_ref.shape, jnp.float32)
            for e in range(count):
                for k in range(picks):
                    keep = jnp.where(tile_smem[e, k] == tile, jnp.float32(1.0), jnp.float32(0.0))
                    total = total + keep * parts[e, k]
            return total

        for j in range(n_exp):
            peer = lax.rem(x + j, n_exp)
            outbox[step, n_exp + peer] = gather(n_exp + peer).astype(jnp.bfloat16)
            pending.append(send(
                outbox.at[step, n_exp + peer], inbox.at[step, n_exp + x], bwd_send.at[step, n_exp + j],
                bwd_recv.at[step, n_exp + x], (after, peer),
            ))
            if j:
                outbox[step, peer] = gather(peer).astype(jnp.bfloat16)
                pending.append(send(
                    outbox.at[step, peer], inbox.at[step, x], bwd_send.at[step, j], bwd_recv.at[step, x], (g, peer)
                ))
        total = gather(x)
        for j in range(1, n_exp):
            slot = lax.rem(x + j, n_exp)
            arrive(inbox, bwd_recv, step, slot)
            total = total + inbox[step, slot].astype(jnp.float32)
        for j in range(n_exp):
            slot = n_exp + j
            arrive(inbox, bwd_recv, step, slot)
            total = total + inbox[step, slot].astype(jnp.float32)
        updated = sky_out[...] + STEP * total
        sky_out[...] = updated
        if step < ITERS - 1:
            window[step + 1, x] = updated.astype(jnp.bfloat16)
            pending += spread(step + 1)

    for copy in pending:
        copy.wait_send()


def shards(
    n_grp, n_exp, sky, observed, intersections, resample_index, psf_index, resample_table, psf_weights, psf_basis
):
    tiles, bands, rows, width = sky.shape
    count, picks = intersections.shape
    flat = tiles * bands * rows
    slots = 2 * n_exp
    comp = psf_basis.shape[0]
    smem = pl.BlockSpec(memory_space=pltpu.SMEM)
    vmem = pl.BlockSpec(memory_space=pltpu.VMEM)
    sky_out, residual = pl.pallas_call(
        functools.partial(kernel, n_grp, n_exp),
        out_shape=(
            jax.ShapeDtypeStruct((flat, width), jnp.float32),
            jax.ShapeDtypeStruct((count, flat, width), jnp.float32),
        ),
        in_specs=[smem] * 4 + [vmem] * 3 + [pl.BlockSpec(memory_space=pl.ANY)],
        out_specs=(vmem, vmem),
        scratch_shapes=[
            pltpu.VMEM(resample_table.shape, jnp.bfloat16),
            pltpu.VMEM((ITERS, slots, flat, width), jnp.bfloat16),
            pltpu.VMEM((ITERS, slots, flat, width), jnp.bfloat16),
            pltpu.VMEM((ITERS, slots, flat, width), jnp.bfloat16),
            pltpu.VMEM((count, picks, flat, width), jnp.float32),
            pltpu.VMEM((count, width, width), jnp.bfloat16),
            pltpu.VMEM((comp, 2 * LANES), jnp.float32),
            pltpu.SemaphoreType.DMA,
        ]
        + [pltpu.SemaphoreType.DMA((ITERS, slots))] * 4,
        compiler_params=pltpu.CompilerParams(
            collective_id=0, has_side_effects=True, vmem_limit_bytes=48 * 2**20
        ),
    )(
        intersections, resample_index, psf_index, psf_weights, psf_basis,
        sky.reshape(flat, width), observed.reshape(count, flat, width), resample_table,
    )
    return sky_out.reshape(sky.shape), residual.reshape(observed.shape)


def solution(mesh):
    both = ("grp", "exp")
    in_specs = (
        P(both, None, None, None), P(both, None, None, None), P(both, None), P(both, None), P(both), P(), P(), P(),
    )
    out_specs = (P(both, None, None, None), P(both, None, None, None))
    body = functools.partial(shards, mesh.shape["grp"], mesh.shape["exp"])
    return jax.shard_map(body, mesh=mesh, in_specs=in_specs, out_specs=out_specs, check_vma=False)
```

```python
import functools

import jax
import jax.numpy as jnp
from jax import lax
from jax.experimental import pallas as pl
from jax.experimental.pallas import tpu as pltpu
from jax.sharding import PartitionSpec as P

ITERS = 2
STEP = 0.05
LANES = 128
PAD = 64
MESH = pl.DeviceIdType.MESH
NN = (((1,), (0,)), ((), ()))
NT = (((1,), (1,)), ((), ()))


def dot(a, b, dims):
    return lax.dot_general(a, b, dims, preferred_element_type=jnp.float32)


def pad_rows(value, rows):
    short = rows - value.shape[0]
    if not short:
        return value
    return jnp.concatenate([value, jnp.zeros((short, value.shape[1]), value.dtype)], axis=0)


def put(ref, start, value):
    for c in range(ref.shape[0]):
        ref[c, start : start + value.shape[0], :] = value[:, c * LANES : (c + 1) * LANES]


def every(ref, start, size, stride):
    return jnp.concatenate([ref[c, pl.ds(start, size, stride=stride), :] for c in range(ref.shape[0])], axis=1)


def banded(value, band, dims):
    rows, width = value.shape
    blocks = width // LANES
    wide = jnp.concatenate([value, jnp.zeros((rows, 2 * PAD), jnp.float32)], axis=1)
    wide = pltpu.roll(wide, PAD, 1).astype(jnp.bfloat16)
    stacked = jnp.concatenate([wide[:, j * LANES : (j + 2) * LANES] for j in range(blocks)], axis=0)
    out = dot(stacked, band, dims)
    return jnp.concatenate([out[j * rows : (j + 1) * rows] for j in range(blocks)], axis=1)


def kernel(n_grp, n_exp, *refs):
    sources, (sky_out, resid_out), held, rest = refs[:8], refs[8:10], refs[10:18], refs[18:]
    tile_smem, res_smem, psf_smem, weights_smem, basis_ref, sky_ref, obs_ref, table = held
    (load_sem, sky_stage, obs_stage, meta, win, obs, back_in, grad_in, grad_out, delta_stage, delta_in,
     res_stage, res_in, taps, wide, mixed, pre, back, folded, grad, state, delta, pick_f, pick_b, band_f, band_b,
     sky_send, sky_recv, meta_send, meta_recv, obs_send, obs_recv, hop_send, hop_recv, grad_send, grad_recv,
     delta_send, delta_recv, res_send, res_recv) = rest
    g = lax.axis_index("grp")
    x = lax.axis_index("exp")
    before = lax.rem(g + n_grp - 1, n_grp)
    after = lax.rem(g + 1, n_grp)
    count, picks = tile_smem.shape
    flat, width = sky_ref.shape
    mats = table.shape[0]
    comp, tap_count = basis_ref.shape
    half = (tap_count - 1) // 2
    rows = flat // n_exp
    padded = sky_stage.shape[1]
    group_exp = count * n_exp
    tiles = 2 * n_exp

    loads = [pltpu.make_async_copy(src, dst, load_sem.at[i]) for i, (src, dst) in enumerate(zip(sources, held))]
    for i in (5, 0, 1, 2, 3, 4, 6, 7):
        loads[i].start()

    barrier = pltpu.get_barrier_semaphore()
    for j in range(1, n_exp):
        pl.semaphore_signal(barrier, inc=1, device_id=(g, lax.rem(x + j, n_exp)), device_id_type=MESH)
    for group in (before, after):
        pl.semaphore_signal(barrier, inc=1, device_id=(group, x), device_id_type=MESH)

    def send(src, dst, send_sem, recv_sem, where):
        copy = pltpu.make_async_remote_copy(
            src_ref=src, dst_ref=dst, send_sem=send_sem, recv_sem=recv_sem, device_id=where, device_id_type=MESH
        )
        copy.start()
        pending.append(copy)

    def arrive(ref, sem):
        pltpu.make_async_copy(ref, ref, sem).wait()

    pending = []
    loads[5].wait()
    for p in range(n_exp):
        sky_stage[p] = pad_rows(sky_ref[p * rows : (p + 1) * rows, :], padded).astype(jnp.bfloat16)
    win[0, x] = sky_stage[x]
    pl.semaphore_wait(barrier, n_exp + 1)
    for j in range(1, n_exp):
        peer = lax.rem(x + j, n_exp)
        send(sky_stage.at[peer], win.at[0, x], sky_send.at[j], sky_recv.at[x], (g, peer))

    for i in (0, 1, 2, 3, 4):
        loads[i].wait()
    taps[...] = jnp.zeros_like(taps)
    taps[:, PAD - half : PAD - half + tap_count] = basis_ref[...]
    lane = lax.broadcasted_iota(jnp.int32, (1, LANES), 1)
    info = []
    for e in range(count):
        fields = jnp.zeros((1, LANES), jnp.float32)
        for k in range(picks):
            fields = jnp.where(lane == k, tile_smem[e, k].astype(jnp.float32), fields)
            fields = jnp.where(lane == picks + k, res_smem[e, k].astype(jnp.float32), fields)
        kern = jnp.zeros((1, 2 * LANES), jnp.float32)
        for c in range(comp):
            kern = kern + weights_smem[c, psf_smem[e]] * taps[c : c + 1, :]
        info.append(jnp.concatenate([fields, kern], axis=1))
    meta[x] = pad_rows(jnp.concatenate(info, axis=0), meta.shape[1])
    for j in range(1, n_exp):
        peer = lax.rem(x + j, n_exp)
        send(meta.at[x], meta.at[x], meta_send.at[j], meta_recv.at[x], (g, peer))

    loads[6].wait()
    for e in range(count):
        whole = obs_ref[e].astype(jnp.float32)
        for p in range(n_exp):
            obs_stage[p, e] = pad_rows(whole[p * rows : (p + 1) * rows, :], padded).astype(jnp.bfloat16)
    obs[x] = obs_stage[x]
    for j in range(1, n_exp):
        peer = lax.rem(x + j, n_exp)
        send(obs_stage.at[peer], obs.at[x], obs_send.at[j], obs_recv.at[x], (g, peer))

    def hop(step):
        send(
            win.at[step, pl.ds(0, n_exp)], win.at[step, pl.ds(n_exp, n_exp)], hop_send.at[step], hop_recv.at[step],
            (before, x),
        )

    for j in range(1, n_exp):
        slot = lax.rem(x + j, n_exp)
        arrive(win.at[0, slot], sky_recv.at[slot])
    hop(0)
    for t in range(n_exp):
        state[t] = win[0, t].astype(jnp.float32)
        delta[t] = jnp.zeros_like(state[t])

    for j in range(1, n_exp):
        slot = lax.rem(x + j, n_exp)
        arrive(meta.at[slot], meta_recv.at[slot])
    info = jnp.concatenate([meta[d, :count, :] for d in range(n_exp)], axis=0)
    fields = info[:, :LANES]
    tile_lane = lax.broadcasted_iota(jnp.int32, (group_exp, LANES), 1).astype(jnp.float32)
    columns = [jnp.broadcast_to(fields[:, k : k + 1], (group_exp, LANES)) for k in range(2 * picks)]
    across = jnp.transpose(pad_rows(fields, LANES))
    tile_row = lax.broadcasted_iota(jnp.int32, (tiles, LANES), 0).astype(jnp.float32)
    spans = [jnp.broadcast_to(across[k : k + 1, :], (tiles, LANES)) for k in range(2 * picks)]
    exists = lax.broadcasted_iota(jnp.int32, (tiles, LANES), 1) < group_exp
    for n in range(mats):
        hits = jnp.zeros((group_exp, LANES), jnp.float32)
        spread = jnp.zeros((tiles, LANES), jnp.float32)
        for k in range(picks):
            hits = hits + jnp.where((columns[picks + k] == n) & (columns[k] == tile_lane), 1.0, 0.0)
            spread = spread + jnp.where((spans[picks + k] == n) & (spans[k] == tile_row) & exists, 1.0, 0.0)
        pick_f[n * group_exp : (n + 1) * group_exp, :] = hits.astype(jnp.bfloat16)
        pick_b[n * tiles : (n + 1) * tiles, :] = spread.astype(jnp.bfloat16)
    for e in range(group_exp):
        kern = info[e : e + 1, LANES:]
        ahead = jnp.broadcast_to(kern, (LANES, 2 * LANES))
        band_f[e] = pltpu.roll(ahead, 0, 1, stride=1, stride_axis=0).astype(jnp.bfloat16)
        moved = jnp.broadcast_to(pltpu.roll(kern, 2 * LANES - 2 * PAD, 1), (2 * LANES, 2 * LANES))
        band_b[e] = pltpu.roll(moved, 0, 1, stride=1, stride_axis=0)[:, :LANES].astype(jnp.bfloat16)

    for j in range(1, n_exp):
        slot = lax.rem(x + j, n_exp)
        arrive(obs.at[slot], obs_recv.at[slot])
    loads[7].wait()

    for step in range(ITERS):
        arrive(win.at[step, pl.ds(n_exp, n_exp)], hop_recv.at[step])
        for t in range(tiles):
            put(wide, t * padded, win[step, t].astype(jnp.float32))
        for r in range(rows):
            line = every(wide, r, tiles, padded).astype(jnp.bfloat16)
            mix = dot(pick_f[:, :tiles], line, NN).astype(jnp.bfloat16)
            for n in range(mats):
                mixed[n, r * group_exp : (r + 1) * group_exp, :] = mix[n * group_exp : (n + 1) * group_exp]
        total = dot(mixed[0], table[0], NN)
        for n in range(1, mats):
            total = total + dot(mixed[n], table[n], NN)
        put(pre, 0, total)

        for d in range(n_exp):
            for k in range(count):
                e = d * count + k
                line = pad_rows(every(pre, e, rows, group_exp), padded)
                residual = obs[d, k].astype(jnp.float32) - banded(line, band_f[e], NT)
                if step == ITERS - 1:
                    res_stage[d, k] = residual.astype(jnp.bfloat16)
                put(back, e * padded, banded(residual, band_b[e], NN))
        if step == ITERS - 1:
            res_in[x] = res_stage[x]
            for j in range(1, n_exp):
                peer = lax.rem(x + j, n_exp)
                send(res_stage.at[peer], res_in.at[x], res_send.at[j], res_recv.at[x], (g, peer))

        for r in range(rows):
            line = every(back, r, group_exp, padded).astype(jnp.bfloat16)
            fold = dot(pick_b[:, :group_exp], line, NN)
            for n in range(mats):
                folded[n, r * tiles : (r + 1) * tiles, :] = fold[n * tiles : (n + 1) * tiles]
        total = dot(folded[0].astype(jnp.bfloat16), table[0], NT)
        for n in range(1, mats):
            total = total + dot(folded[n].astype(jnp.bfloat16), table[n], NT)
        put(grad, 0, total)

        for t in range(n_exp):
            line = pad_rows(every(grad, n_exp + t, rows, tiles), padded)
            grad_out[step, t] = line.astype(jnp.bfloat16)
        send(grad_out.at[step], grad_in.at[step], grad_send.at[step], grad_recv.at[step], (after, x))
        arrive(grad_in.at[step], grad_recv.at[step])
        for t in range(n_exp):
            line = pad_rows(every(grad, t, rows, tiles), padded)
            update = STEP * (line + grad_in[step, t].astype(jnp.float32))
            if step < ITERS - 1:
                state[t] = state[t] + update
                delta[t] = delta[t] + update
                win[step + 1, t] = state[t].astype(jnp.bfloat16)
            else:
                delta_stage[t] = (delta[t] + update).astype(jnp.bfloat16)
        if step < ITERS - 1:
            hop(step + 1)

    delta_in[x] = delta_stage[x]
    for j in range(1, n_exp):
        peer = lax.rem(x + j, n_exp)
        send(delta_stage.at[peer], delta_in.at[x], delta_send.at[j], delta_recv.at[x], (g, peer))
    for j in range(1, n_exp):
        slot = lax.rem(x + j, n_exp)
        arrive(res_in.at[slot], res_recv.at[slot])
    for p in range(n_exp):
        span = slice(p * rows, (p + 1) * rows)
        for e in range(count):
            resid_out[e, span, :] = res_in[p, e].astype(jnp.float32)[:rows]
    for j in range(1, n_exp):
        slot = lax.rem(x + j, n_exp)
        arrive(delta_in.at[slot], delta_recv.at[slot])
    for p in range(n_exp):
        span = slice(p * rows, (p + 1) * rows)
        sky_out[span, :] = sky_ref[span, :] + delta_in[p].astype(jnp.float32)[:rows]
    for copy in pending:
        copy.wait_send()


def shards(
    n_grp, n_exp, sky, observed, intersections, resample_index, psf_index, resample_table, psf_weights, psf_basis
):
    bands, lines, width = sky.shape[1:]
    count = intersections.shape[0]
    flat = bands * lines
    rows = flat // n_exp
    padded = -(-rows // 16) * 16
    group_exp = count * n_exp
    tiles = 2 * n_exp
    mats = resample_table.shape[0]
    comp = psf_basis.shape[0]
    operands = (
        intersections, resample_index, psf_index, psf_weights.T, psf_basis,
        sky.reshape(flat, width), observed.reshape(count, flat, width), resample_table,
    )
    vmem = pl.BlockSpec(memory_space=pltpu.VMEM)
    half, full = jnp.bfloat16, jnp.float32
    sems = pltpu.SemaphoreType.DMA
    scratch = [
        *((pltpu.SMEM if i < 4 else pltpu.VMEM)(operand.shape, operand.dtype) for i, operand in enumerate(operands)),
        sems((len(operands),)),
        pltpu.VMEM((n_exp, padded, width), half),
        pltpu.VMEM((n_exp, count, padded, width), half),
        pltpu.VMEM((n_exp, 8, 3 * LANES), full),
        pltpu.VMEM((ITERS, tiles, padded, width), half),
        pltpu.VMEM((n_exp, count, padded, width), half),
        pltpu.VMEM((8, LANES), full),
        pltpu.VMEM((ITERS, n_exp, padded, width), half),
        pltpu.VMEM((ITERS, n_exp, padded, width), half),
        pltpu.VMEM((n_exp, padded, width), half),
        pltpu.VMEM((n_exp, padded, width), half),
        pltpu.VMEM((n_exp, count, padded, width), half),
        pltpu.VMEM((n_exp, count, padded, width), half),
        pltpu.VMEM((comp, 2 * LANES), full),
        pltpu.VMEM((width // LANES, tiles * padded, LANES), full),
        pltpu.VMEM((mats, rows * group_exp, width), half),
        pltpu.VMEM((width // LANES, rows * group_exp, LANES), full),
        pltpu.VMEM((width // LANES, group_exp * padded, LANES), full),
        pltpu.VMEM((mats, rows * tiles, width), full),
        pltpu.VMEM((width // LANES, rows * tiles, LANES), full),
        pltpu.VMEM((n_exp, padded, width), full),
        pltpu.VMEM((n_exp, padded, width), full),
        pltpu.VMEM((mats * group_exp, LANES), half),
        pltpu.VMEM((mats * tiles, LANES), half),
        pltpu.VMEM((group_exp, LANES, 2 * LANES), half),
        pltpu.VMEM((group_exp, 2 * LANES, LANES), half),
        *([sems((n_exp,))] * 6),
        *([sems((ITERS,))] * 4),
        *([sems((n_exp,))] * 4),
    ]
    sky_out, residual = pl.pallas_call(
        functools.partial(kernel, n_grp, n_exp),
        out_shape=(
            jax.ShapeDtypeStruct((flat, width), full),
            jax.ShapeDtypeStruct((count, flat, width), full),
        ),
        in_specs=[pl.BlockSpec(memory_space=pltpu.HBM)] * len(operands),
        out_specs=(vmem, vmem),
        scratch_shapes=scratch,
        compiler_params=pltpu.CompilerParams(
            collective_id=0, has_side_effects=True, vmem_limit_bytes=64 * 2**20
        ),
    )(*operands)
    return sky_out.reshape(sky.shape), residual.reshape(observed.shape)


def solution(mesh):
    both = ("grp", "exp")
    in_specs = (
        P(both, None, None, None), P(both, None, None, None), P(both, None), P(both, None), P(both), P(), P(), P(),
    )
    out_specs = (P(both, None, None, None), P(both, None, None, None))
    body = functools.partial(shards, mesh.shape["grp"], mesh.shape["exp"])
    return jax.shard_map(body, mesh=mesh, in_specs=in_specs, out_specs=out_specs, check_vma=False)
```

```python
import functools

import jax
import jax.numpy as jnp
from jax import lax
from jax.experimental import pallas as pl
from jax.experimental.pallas import tpu as pltpu
from jax.sharding import PartitionSpec as P

ITERS = 2
STEP = 0.05
LANES = 128
PAD = 64
MESH = pl.DeviceIdType.MESH
NN = (((1,), (0,)), ((), ()))
NT = (((1,), (1,)), ((), ()))


def dot(a, b, dims):
    return lax.dot_general(a, b, dims, preferred_element_type=jnp.float32)


def pad_rows(value, rows):
    short = rows - value.shape[0]
    if not short:
        return value
    return jnp.concatenate([value, jnp.zeros((short, value.shape[1]), value.dtype)], axis=0)


def put(ref, start, value):
    for c in range(ref.shape[0]):
        ref[c, start : start + value.shape[0], :] = value[:, c * LANES : (c + 1) * LANES]


def every(ref, start, size, stride):
    return jnp.concatenate([ref[c, pl.ds(start, size, stride=stride), :] for c in range(ref.shape[0])], axis=1)


def banded(value, band, dims):
    rows, width = value.shape
    blocks = width // LANES
    wide = jnp.concatenate([value, jnp.zeros((rows, 2 * PAD), jnp.float32)], axis=1)
    wide = pltpu.roll(wide, PAD, 1).astype(jnp.bfloat16)
    stacked = jnp.concatenate([wide[:, j * LANES : (j + 2) * LANES] for j in range(blocks)], axis=0)
    out = dot(stacked, band, dims)
    return jnp.concatenate([out[j * rows : (j + 1) * rows] for j in range(blocks)], axis=1)


def kernel(n_grp, n_exp, *refs):
    sources, (sky_out, resid_out), held, rest = refs[:8], refs[8:10], refs[10:18], refs[18:]
    tile_smem, res_smem, psf_smem, weights_smem, basis_ref, sky_ref, obs_ref, table = held
    (load_sem, sky_stage, obs_stage, meta, win, obs, back_in, grad_in, grad_out, delta_stage, delta_in,
     res_stage, res_in, taps, wide, mixed, pre, back, folded, grad, state, delta, pick_f, pick_b, band_f, band_b,
     sky_send, sky_recv, meta_send, meta_recv, obs_send, obs_recv, hop_send, hop_recv, grad_send, grad_recv,
     delta_send, delta_recv, res_send, res_recv,
     next_send, next_recv, last_send, last_recv, last_stage, last_in) = rest
    g = lax.axis_index("grp")
    x = lax.axis_index("exp")
    before = lax.rem(g + n_grp - 1, n_grp)
    after = lax.rem(g + 1, n_grp)
    count, picks = tile_smem.shape
    flat, width = sky_ref.shape
    mats = table.shape[0]
    comp, tap_count = basis_ref.shape
    half = (tap_count - 1) // 2
    rows = flat // n_exp
    padded = sky_stage.shape[1]
    group_exp = count * n_exp
    tiles = 2 * n_exp

    loads = [pltpu.make_async_copy(src, dst, load_sem.at[i]) for i, (src, dst) in enumerate(zip(sources, held))]
    for i in (5, 0, 1, 2, 3, 4, 6, 7):
        loads[i].start()

    barrier = pltpu.get_barrier_semaphore()
    for j in range(n_exp):
        peer = lax.rem(x + j, n_exp)
        for group in (before, after, g) if j else (before, after):
            pl.semaphore_signal(barrier, inc=1, device_id=(group, peer), device_id_type=MESH)

    def send(src, dst, send_sem, recv_sem, where):
        copy = pltpu.make_async_remote_copy(
            src_ref=src, dst_ref=dst, send_sem=send_sem, recv_sem=recv_sem, device_id=where, device_id_type=MESH
        )
        copy.start()
        pending.append(copy)

    def arrive(ref, sem):
        pltpu.make_async_copy(ref, ref, sem).wait()

    pending = []
    loads[5].wait()
    for p in range(n_exp):
        sky_stage[p] = pad_rows(sky_ref[p * rows : (p + 1) * rows, :], padded).astype(jnp.bfloat16)
    win[0, x] = sky_stage[x]
    pl.semaphore_wait(barrier, 3 * n_exp - 1)
    for j in range(n_exp):
        peer = lax.rem(x + j, n_exp)
        send(sky_stage.at[peer], win.at[0, n_exp + x], next_send.at[j], next_recv.at[x], (before, peer))
    for j in range(1, n_exp):
        peer = lax.rem(x + j, n_exp)
        send(sky_stage.at[peer], win.at[0, x], sky_send.at[j], sky_recv.at[x], (g, peer))

    for i in (0, 1, 2, 3, 4):
        loads[i].wait()
    taps[...] = jnp.zeros_like(taps)
    taps[:, PAD - half : PAD - half + tap_count] = basis_ref[...]
    lane = lax.broadcasted_iota(jnp.int32, (1, LANES), 1)
    info = []
    for e in range(count):
        fields = jnp.zeros((1, LANES), jnp.float32)
        for k in range(picks):
            fields = jnp.where(lane == k, tile_smem[e, k].astype(jnp.float32), fields)
            fields = jnp.where(lane == picks + k, res_smem[e, k].astype(jnp.float32), fields)
        kern = jnp.zeros((1, 2 * LANES), jnp.float32)
        for c in range(comp):
            kern = kern + weights_smem[c, psf_smem[e]] * taps[c : c + 1, :]
        info.append(jnp.concatenate([fields, kern], axis=1))
    meta[x] = pad_rows(jnp.concatenate(info, axis=0), meta.shape[1])
    for j in range(1, n_exp):
        peer = lax.rem(x + j, n_exp)
        send(meta.at[x], meta.at[x], meta_send.at[j], meta_recv.at[x], (g, peer))

    loads[6].wait()
    for e in range(count):
        whole = obs_ref[e].astype(jnp.float32)
        for p in range(n_exp):
            obs_stage[p, e] = pad_rows(whole[p * rows : (p + 1) * rows, :], padded).astype(jnp.bfloat16)
    obs[x] = obs_stage[x]
    for j in range(1, n_exp):
        peer = lax.rem(x + j, n_exp)
        send(obs_stage.at[peer], obs.at[x], obs_send.at[j], obs_recv.at[x], (g, peer))

    for j in range(1, n_exp):
        slot = lax.rem(x + j, n_exp)
        arrive(meta.at[slot], meta_recv.at[slot])
    info = jnp.concatenate([meta[d, :count, :] for d in range(n_exp)], axis=0)
    fields = info[:, :LANES]
    tile_lane = lax.broadcasted_iota(jnp.int32, (group_exp, LANES), 1).astype(jnp.float32)
    columns = [jnp.broadcast_to(fields[:, k : k + 1], (group_exp, LANES)) for k in range(2 * picks)]
    across = jnp.transpose(pad_rows(fields, LANES))
    tile_row = lax.broadcasted_iota(jnp.int32, (tiles, LANES), 0).astype(jnp.float32)
    spans = [jnp.broadcast_to(across[k : k + 1, :], (tiles, LANES)) for k in range(2 * picks)]
    exists = lax.broadcasted_iota(jnp.int32, (tiles, LANES), 1) < group_exp
    for n in range(mats):
        hits = jnp.zeros((group_exp, LANES), jnp.float32)
        spread = jnp.zeros((tiles, LANES), jnp.float32)
        for k in range(picks):
            hits = hits + jnp.where((columns[picks + k] == n) & (columns[k] == tile_lane), 1.0, 0.0)
            spread = spread + jnp.where((spans[picks + k] == n) & (spans[k] == tile_row) & exists, 1.0, 0.0)
        pick_f[n * group_exp : (n + 1) * group_exp, :] = hits.astype(jnp.bfloat16)
        pick_b[n * tiles : (n + 1) * tiles, :] = spread.astype(jnp.bfloat16)
    for e in range(group_exp):
        kern = info[e : e + 1, LANES:]
        ahead = jnp.broadcast_to(kern, (LANES, 2 * LANES))
        band_f[e] = pltpu.roll(ahead, 0, 1, stride=1, stride_axis=0).astype(jnp.bfloat16)
        moved = jnp.broadcast_to(pltpu.roll(kern, 2 * LANES - 2 * PAD, 1), (2 * LANES, 2 * LANES))
        band_b[e] = pltpu.roll(moved, 0, 1, stride=1, stride_axis=0)[:, :LANES].astype(jnp.bfloat16)

    for j in range(1, n_exp):
        slot = lax.rem(x + j, n_exp)
        arrive(obs.at[slot], obs_recv.at[slot])
    loads[7].wait()
    for j in range(1, n_exp):
        slot = lax.rem(x + j, n_exp)
        arrive(win.at[0, slot], sky_recv.at[slot])
    for j in range(n_exp):
        arrive(win.at[0, n_exp + j], next_recv.at[j])
    for t in range(tiles):
        state[t] = win[0, t].astype(jnp.float32)
    for t in range(n_exp):
        delta[t] = jnp.zeros_like(state[t])

    for step in range(ITERS):
        for t in range(tiles):
            put(wide, t * padded, state[t])
        for r in range(rows):
            line = every(wide, r, tiles, padded).astype(jnp.bfloat16)
            mix = dot(pick_f[:, :tiles], line, NN).astype(jnp.bfloat16)
            for n in range(mats):
                mixed[n, r * group_exp : (r + 1) * group_exp, :] = mix[n * group_exp : (n + 1) * group_exp]
        total = dot(mixed[0], table[0], NN)
        for n in range(1, mats):
            total = total + dot(mixed[n], table[n], NN)
        put(pre, 0, total)

        for d in range(n_exp):
            for k in range(count):
                e = d * count + k
                line = pad_rows(every(pre, e, rows, group_exp), padded)
                residual = obs[d, k].astype(jnp.float32) - banded(line, band_f[e], NT)
                if step == ITERS - 1:
                    res_stage[d, k] = residual.astype(jnp.bfloat16)
                put(back, e * padded, banded(residual, band_b[e], NN))
        if step == ITERS - 1:
            res_in[x] = res_stage[x]
            for j in range(1, n_exp):
                peer = lax.rem(x + j, n_exp)
                send(res_stage.at[peer], res_in.at[x], res_send.at[j], res_recv.at[x], (g, peer))

        for r in range(rows):
            line = every(back, r, group_exp, padded).astype(jnp.bfloat16)
            fold = dot(pick_b[:, :group_exp], line, NN)
            for n in range(mats):
                folded[n, r * tiles : (r + 1) * tiles, :] = fold[n * tiles : (n + 1) * tiles]
        total = dot(folded[0].astype(jnp.bfloat16), table[0], NT)
        for n in range(1, mats):
            total = total + dot(folded[n].astype(jnp.bfloat16), table[n], NT)
        put(grad, 0, total)

        parts = [pad_rows(every(grad, t, rows, tiles), padded) for t in range(tiles)]
        if step < ITERS - 1:
            for t in range(tiles):
                grad_out[step, t] = parts[t].astype(jnp.bfloat16)
            own, following = pl.ds(0, n_exp), pl.ds(n_exp, n_exp)
            send(grad_out.at[step, following], grad_in.at[step, own], grad_send.at[step], grad_recv.at[step], (after, x))
            send(grad_out.at[step, own], grad_in.at[step, following], hop_send.at[step], hop_recv.at[step], (before, x))
            arrive(grad_in.at[step, own], grad_recv.at[step])
            arrive(grad_in.at[step, following], hop_recv.at[step])
            for t in range(tiles):
                update = STEP * (parts[t] + grad_in[step, t].astype(jnp.float32))
                state[t] = state[t] + update
                if t < n_exp:
                    delta[t] = delta[t] + update
        else:
            for t in range(n_exp):
                last_stage[t] = (STEP * parts[n_exp + t]).astype(jnp.bfloat16)
                delta_stage[t] = (delta[t] + STEP * parts[t]).astype(jnp.bfloat16)

    for j in range(n_exp):
        peer = lax.rem(x + j, n_exp)
        send(last_stage.at[peer], last_in.at[x], last_send.at[j], last_recv.at[x], (after, peer))
    delta_in[x] = delta_stage[x]
    for j in range(1, n_exp):
        peer = lax.rem(x + j, n_exp)
        send(delta_stage.at[peer], delta_in.at[x], delta_send.at[j], delta_recv.at[x], (g, peer))
    for j in range(1, n_exp):
        slot = lax.rem(x + j, n_exp)
        arrive(res_in.at[slot], res_recv.at[slot])
    for p in range(n_exp):
        span = slice(p * rows, (p + 1) * rows)
        for e in range(count):
            resid_out[e, span, :] = res_in[p, e].astype(jnp.float32)[:rows]
    for j in range(1, n_exp):
        slot = lax.rem(x + j, n_exp)
        arrive(delta_in.at[slot], delta_recv.at[slot])
    for j in range(n_exp):
        arrive(last_in.at[j], last_recv.at[j])
    for p in range(n_exp):
        span = slice(p * rows, (p + 1) * rows)
        sky_out[span, :] = sky_ref[span, :] + (delta_in[p].astype(jnp.float32) + last_in[p].astype(jnp.float32))[:rows]
    for copy in pending:
        copy.wait_send()


def shards(
    n_grp, n_exp, sky, observed, intersections, resample_index, psf_index, resample_table, psf_weights, psf_basis
):
    bands, lines, width = sky.shape[1:]
    count = intersections.shape[0]
    flat = bands * lines
    rows = flat // n_exp
    padded = -(-rows // 16) * 16
    group_exp = count * n_exp
    tiles = 2 * n_exp
    mats = resample_table.shape[0]
    comp = psf_basis.shape[0]
    operands = (
        intersections, resample_index, psf_index, psf_weights.T, psf_basis,
        sky.reshape(flat, width), observed.reshape(count, flat, width), resample_table,
    )
    vmem = pl.BlockSpec(memory_space=pltpu.VMEM)
    half, full = jnp.bfloat16, jnp.float32
    sems = pltpu.SemaphoreType.DMA
    scratch = [
        *((pltpu.SMEM if i < 4 else pltpu.VMEM)(operand.shape, operand.dtype) for i, operand in enumerate(operands)),
        sems((len(operands),)),
        pltpu.VMEM((n_exp, padded, width), half),
        pltpu.VMEM((n_exp, count, padded, width), half),
        pltpu.VMEM((n_exp, 8, 3 * LANES), full),
        pltpu.VMEM((1, tiles, padded, width), half),
        pltpu.VMEM((n_exp, count, padded, width), half),
        pltpu.VMEM((8, LANES), full),
        pltpu.VMEM((ITERS, tiles, padded, width), half),
        pltpu.VMEM((ITERS, tiles, padded, width), half),
        pltpu.VMEM((n_exp, padded, width), half),
        pltpu.VMEM((n_exp, padded, width), half),
        pltpu.VMEM((n_exp, count, padded, width), half),
        pltpu.VMEM((n_exp, count, padded, width), half),
        pltpu.VMEM((comp, 2 * LANES), full),
        pltpu.VMEM((width // LANES, tiles * padded, LANES), full),
        pltpu.VMEM((mats, rows * group_exp, width), half),
        pltpu.VMEM((width // LANES, rows * group_exp, LANES), full),
        pltpu.VMEM((width // LANES, group_exp * padded, LANES), full),
        pltpu.VMEM((mats, rows * tiles, width), full),
        pltpu.VMEM((width // LANES, rows * tiles, LANES), full),
        pltpu.VMEM((tiles, padded, width), full),
        pltpu.VMEM((n_exp, padded, width), full),
        pltpu.VMEM((mats * group_exp, LANES), half),
        pltpu.VMEM((mats * tiles, LANES), half),
        pltpu.VMEM((group_exp, LANES, 2 * LANES), half),
        pltpu.VMEM((group_exp, 2 * LANES, LANES), half),
        *([sems((n_exp,))] * 6),
        *([sems((ITERS,))] * 4),
        *([sems((n_exp,))] * 8),
        *([pltpu.VMEM((n_exp, padded, width), half)] * 2),
    ]
    sky_out, residual = pl.pallas_call(
        functools.partial(kernel, n_grp, n_exp),
        out_shape=(
            jax.ShapeDtypeStruct((flat, width), full),
            jax.ShapeDtypeStruct((count, flat, width), full),
        ),
        in_specs=[pl.BlockSpec(memory_space=pltpu.HBM)] * len(operands),
        out_specs=(vmem, vmem),
        scratch_shapes=scratch,
        compiler_params=pltpu.CompilerParams(
            collective_id=0, has_side_effects=True, vmem_limit_bytes=64 * 2**20
        ),
    )(*operands)
    return sky_out.reshape(sky.shape), residual.reshape(observed.shape)


def solution(mesh):
    both = ("grp", "exp")
    in_specs = (
        P(both, None, None, None), P(both, None, None, None), P(both, None), P(both, None), P(both), P(), P(), P(),
    )
    out_specs = (P(both, None, None, None), P(both, None, None, None))
    body = functools.partial(shards, mesh.shape["grp"], mesh.shape["exp"])
    return jax.shard_map(body, mesh=mesh, in_specs=in_specs, out_specs=out_specs, check_vma=False)
```

```python
import functools

import jax
import jax.numpy as jnp
from jax import lax
from jax.experimental import pallas as pl
from jax.experimental.pallas import tpu as pltpu
from jax.sharding import PartitionSpec as P

ITERS = 2
STEP = 0.05
LANES = 128
PAD = 64
MESH = pl.DeviceIdType.MESH
NN = (((1,), (0,)), ((), ()))
NT = (((1,), (1,)), ((), ()))


def dot(a, b, dims):
    return lax.dot_general(a, b, dims, preferred_element_type=jnp.float32)


def pad_rows(value, rows):
    short = rows - value.shape[0]
    if not short:
        return value
    return jnp.concatenate([value, jnp.zeros((short, value.shape[1]), value.dtype)], axis=0)


def put(ref, start, value):
    for c in range(ref.shape[0]):
        ref[c, start : start + value.shape[0], :] = value[:, c * LANES : (c + 1) * LANES]


def every(ref, start, size, stride):
    return jnp.concatenate([ref[c, pl.ds(start, size, stride=stride), :] for c in range(ref.shape[0])], axis=1)


def banded(value, band, dims):
    rows, width = value.shape
    blocks = width // LANES
    wide = jnp.concatenate([value, jnp.zeros((rows, 2 * PAD), jnp.float32)], axis=1)
    wide = pltpu.roll(wide, PAD, 1).astype(jnp.bfloat16)
    stacked = jnp.concatenate([wide[:, j * LANES : (j + 2) * LANES] for j in range(blocks)], axis=0)
    out = dot(stacked, band, dims)
    return jnp.concatenate([out[j * rows : (j + 1) * rows] for j in range(blocks)], axis=1)


def kernel(n_grp, n_exp, *refs):
    sources, (sky_out, resid_out), held, rest = refs[:8], refs[8:10], refs[10:18], refs[18:]
    tile_smem, res_smem, psf_smem, weights_smem, basis_ref, sky_ref, obs_ref, table = held
    (load_sem, sky_stage, obs_stage, meta, win, obs, back_in, grad_in, grad_out, delta_stage, delta_in,
     res_stage, res_in, taps, wide, mixed, pre, back, folded, grad, state, delta, pick_f, pick_b, band_f, band_b,
     sky_send, sky_recv, meta_send, meta_recv, obs_send, obs_recv, hop_send, hop_recv, grad_send, grad_recv,
     delta_send, delta_recv, res_send, res_recv,
     next_send, next_recv, last_send, last_recv, last_stage, last_in) = rest
    g = lax.axis_index("grp")
    x = lax.axis_index("exp")
    before = lax.rem(g + n_grp - 1, n_grp)
    after = lax.rem(g + 1, n_grp)
    count, picks = tile_smem.shape
    flat, width = sky_ref.shape
    mats = table.shape[0]
    comp, tap_count = basis_ref.shape
    half = (tap_count - 1) // 2
    rows = flat // n_exp
    padded = sky_stage.shape[1]
    group_exp = count * n_exp
    tiles = 2 * n_exp

    loads = [pltpu.make_async_copy(src, dst, load_sem.at[i]) for i, (src, dst) in enumerate(zip(sources, held))]
    for i in (5, 0, 1, 2, 3, 4, 6, 7):
        loads[i].start()

    barrier = pltpu.get_barrier_semaphore()
    for j in range(n_exp):
        peer = lax.rem(x + j, n_exp)
        for group in (before, after, g) if j else (before, after):
            pl.semaphore_signal(barrier, inc=1, device_id=(group, peer), device_id_type=MESH)

    def send(src, dst, send_sem, recv_sem, where):
        copy = pltpu.make_async_remote_copy(
            src_ref=src, dst_ref=dst, send_sem=send_sem, recv_sem=recv_sem, device_id=where, device_id_type=MESH
        )
        copy.start()
        pending.append(copy)

    def arrive(ref, sem):
        pltpu.make_async_copy(ref, ref, sem).wait()

    pending = []
    loads[5].wait()
    for p in range(n_exp):
        sky_stage[p] = pad_rows(sky_ref[p * rows : (p + 1) * rows, :], padded).astype(jnp.bfloat16)
    win[0, x] = sky_stage[x]
    for i in (0, 1, 2, 3, 4):
        loads[i].wait()
    taps[...] = jnp.zeros_like(taps)
    taps[:, PAD - half : PAD - half + tap_count] = basis_ref[...]
    lane = lax.broadcasted_iota(jnp.int32, (1, LANES), 1)
    info = []
    for e in range(count):
        fields = jnp.zeros((1, LANES), jnp.float32)
        for k in range(picks):
            fields = jnp.where(lane == k, tile_smem[e, k].astype(jnp.float32), fields)
            fields = jnp.where(lane == picks + k, res_smem[e, k].astype(jnp.float32), fields)
        kern = jnp.zeros((1, 2 * LANES), jnp.float32)
        for c in range(comp):
            kern = kern + weights_smem[c, psf_smem[e]] * taps[c : c + 1, :]
        info.append(jnp.concatenate([fields, kern], axis=1))
    meta[x] = pad_rows(jnp.concatenate(info, axis=0), meta.shape[1])

    loads[6].wait()
    for e in range(count):
        whole = obs_ref[e].astype(jnp.float32)
        for p in range(n_exp):
            obs_stage[p, e] = pad_rows(whole[p * rows : (p + 1) * rows, :], padded).astype(jnp.bfloat16)
    obs[x] = obs_stage[x]
    pl.semaphore_wait(barrier, 3 * n_exp - 1)
    for j in range(n_exp):
        peer = lax.rem(x + j, n_exp)
        send(sky_stage.at[peer], win.at[0, n_exp + x], next_send.at[j], next_recv.at[x], (before, peer))
    for j in range(1, n_exp):
        peer = lax.rem(x + j, n_exp)
        send(sky_stage.at[peer], win.at[0, x], sky_send.at[j], sky_recv.at[x], (g, peer))
    for j in range(1, n_exp):
        peer = lax.rem(x + j, n_exp)
        send(meta.at[x], meta.at[x], meta_send.at[j], meta_recv.at[x], (g, peer))
    for j in range(1, n_exp):
        peer = lax.rem(x + j, n_exp)
        send(obs_stage.at[peer], obs.at[x], obs_send.at[j], obs_recv.at[x], (g, peer))

    for j in range(1, n_exp):
        slot = lax.rem(x + j, n_exp)
        arrive(meta.at[slot], meta_recv.at[slot])
    info = jnp.concatenate([meta[d, :count, :] for d in range(n_exp)], axis=0)
    fields = info[:, :LANES]
    tile_lane = lax.broadcasted_iota(jnp.int32, (group_exp, LANES), 1).astype(jnp.float32)
    columns = [jnp.broadcast_to(fields[:, k : k + 1], (group_exp, LANES)) for k in range(2 * picks)]
    across = jnp.transpose(pad_rows(fields, LANES))
    tile_row = lax.broadcasted_iota(jnp.int32, (tiles, LANES), 0).astype(jnp.float32)
    spans = [jnp.broadcast_to(across[k : k + 1, :], (tiles, LANES)) for k in range(2 * picks)]
    exists = lax.broadcasted_iota(jnp.int32, (tiles, LANES), 1) < group_exp
    for n in range(mats):
        hits = jnp.zeros((group_exp, LANES), jnp.float32)
        spread = jnp.zeros((tiles, LANES), jnp.float32)
        for k in range(picks):
            hits = hits + jnp.where((columns[picks + k] == n) & (columns[k] == tile_lane), 1.0, 0.0)
            spread = spread + jnp.where((spans[picks + k] == n) & (spans[k] == tile_row) & exists, 1.0, 0.0)
        pick_f[n * group_exp : (n + 1) * group_exp, :] = hits.astype(jnp.bfloat16)
        pick_b[n * tiles : (n + 1) * tiles, :] = spread.astype(jnp.bfloat16)
    for e in range(group_exp):
        kern = info[e : e + 1, LANES:]
        ahead = jnp.broadcast_to(kern, (LANES, 2 * LANES))
        band_f[e] = pltpu.roll(ahead, 0, 1, stride=1, stride_axis=0).astype(jnp.bfloat16)
        moved = jnp.broadcast_to(pltpu.roll(kern, 2 * LANES - 2 * PAD, 1), (2 * LANES, 2 * LANES))
        band_b[e] = pltpu.roll(moved, 0, 1, stride=1, stride_axis=0)[:, :LANES].astype(jnp.bfloat16)

    for j in range(1, n_exp):
        slot = lax.rem(x + j, n_exp)
        arrive(obs.at[slot], obs_recv.at[slot])
    loads[7].wait()
    for j in range(1, n_exp):
        slot = lax.rem(x + j, n_exp)
        arrive(win.at[0, slot], sky_recv.at[slot])
    for j in range(n_exp):
        arrive(win.at[0, n_exp + j], next_recv.at[j])
    for t in range(tiles):
        state[t] = win[0, t].astype(jnp.float32)
    for t in range(n_exp):
        delta[t] = jnp.zeros_like(state[t])

    for step in range(ITERS):
        for t in range(tiles):
            put(wide, t * padded, state[t])
        for r in range(rows):
            line = every(wide, r, tiles, padded).astype(jnp.bfloat16)
            mix = dot(pick_f[:, :tiles], line, NN).astype(jnp.bfloat16)
            for n in range(mats):
                mixed[n, r * group_exp : (r + 1) * group_exp, :] = mix[n * group_exp : (n + 1) * group_exp]
        total = dot(mixed[0], table[0], NN)
        for n in range(1, mats):
            total = total + dot(mixed[n], table[n], NN)
        put(pre, 0, total)

        for d in range(n_exp):
            for k in range(count):
                e = d * count + k
                line = pad_rows(every(pre, e, rows, group_exp), padded)
                residual = obs[d, k].astype(jnp.float32) - banded(line, band_f[e], NT)
                if step == ITERS - 1:
                    res_stage[d, k] = residual.astype(jnp.bfloat16)
                put(back, e * padded, banded(residual, band_b[e], NN))
        if step == ITERS - 1:
            res_in[x] = res_stage[x]
            for j in range(1, n_exp):
                peer = lax.rem(x + j, n_exp)
                send(res_stage.at[peer], res_in.at[x], res_send.at[j], res_recv.at[x], (g, peer))

        for r in range(rows):
            line = every(back, r, group_exp, padded).astype(jnp.bfloat16)
            fold = dot(pick_b[:, :group_exp], line, NN)
            for n in range(mats):
                folded[n, r * tiles : (r + 1) * tiles, :] = fold[n * tiles : (n + 1) * tiles]
        total = dot(folded[0].astype(jnp.bfloat16), table[0], NT)
        for n in range(1, mats):
            total = total + dot(folded[n].astype(jnp.bfloat16), table[n], NT)
        put(grad, 0, total)

        parts = [pad_rows(every(grad, t, rows, tiles), padded) for t in range(tiles)]
        if step < ITERS - 1:
            for t in range(tiles):
                grad_out[step, t] = parts[t].astype(jnp.bfloat16)
            own, following = pl.ds(0, n_exp), pl.ds(n_exp, n_exp)
            send(grad_out.at[step, following], grad_in.at[step, own], grad_send.at[step], grad_recv.at[step], (after, x))
            send(grad_out.at[step, own], grad_in.at[step, following], hop_send.at[step], hop_recv.at[step], (before, x))
            arrive(grad_in.at[step, own], grad_recv.at[step])
            arrive(grad_in.at[step, following], hop_recv.at[step])
            for t in range(tiles):
                update = STEP * (parts[t] + grad_in[step, t].astype(jnp.float32))
                state[t] = state[t] + update
                if t < n_exp:
                    delta[t] = delta[t] + update
        else:
            for t in range(n_exp):
                last_stage[t] = (STEP * parts[n_exp + t]).astype(jnp.bfloat16)
                delta_stage[t] = (delta[t] + STEP * parts[t]).astype(jnp.bfloat16)

    for j in range(n_exp):
        peer = lax.rem(x + j, n_exp)
        send(last_stage.at[peer], last_in.at[x], last_send.at[j], last_recv.at[x], (after, peer))
    delta_in[x] = delta_stage[x]
    for j in range(1, n_exp):
        peer = lax.rem(x + j, n_exp)
        send(delta_stage.at[peer], delta_in.at[x], delta_send.at[j], delta_recv.at[x], (g, peer))
    for j in range(1, n_exp):
        slot = lax.rem(x + j, n_exp)
        arrive(res_in.at[slot], res_recv.at[slot])
    for p in range(n_exp):
        span = slice(p * rows, (p + 1) * rows)
        for e in range(count):
            resid_out[e, span, :] = res_in[p, e].astype(jnp.float32)[:rows]
    for j in range(1, n_exp):
        slot = lax.rem(x + j, n_exp)
        arrive(delta_in.at[slot], delta_recv.at[slot])
    for j in range(n_exp):
        arrive(last_in.at[j], last_recv.at[j])
    for p in range(n_exp):
        span = slice(p * rows, (p + 1) * rows)
        sky_out[span, :] = sky_ref[span, :] + (delta_in[p].astype(jnp.float32) + last_in[p].astype(jnp.float32))[:rows]
    for copy in pending:
        copy.wait_send()


def shards(
    n_grp, n_exp, sky, observed, intersections, resample_index, psf_index, resample_table, psf_weights, psf_basis
):
    bands, lines, width = sky.shape[1:]
    count = intersections.shape[0]
    flat = bands * lines
    rows = flat // n_exp
    padded = -(-rows // 16) * 16
    group_exp = count * n_exp
    tiles = 2 * n_exp
    mats = resample_table.shape[0]
    comp = psf_basis.shape[0]
    operands = (
        intersections, resample_index, psf_index, psf_weights.T, psf_basis,
        sky.reshape(flat, width), observed.reshape(count, flat, width), resample_table,
    )
    vmem = pl.BlockSpec(memory_space=pltpu.VMEM)
    half, full = jnp.bfloat16, jnp.float32
    sems = pltpu.SemaphoreType.DMA
    scratch = [
        *((pltpu.SMEM if i < 4 else pltpu.VMEM)(operand.shape, operand.dtype) for i, operand in enumerate(operands)),
        sems((len(operands),)),
        pltpu.VMEM((n_exp, padded, width), half),
        pltpu.VMEM((n_exp, count, padded, width), half),
        pltpu.VMEM((n_exp, 8, 3 * LANES), full),
        pltpu.VMEM((1, tiles, padded, width), half),
        pltpu.VMEM((n_exp, count, padded, width), half),
        pltpu.VMEM((8, LANES), full),
        pltpu.VMEM((ITERS, tiles, padded, width), half),
        pltpu.VMEM((ITERS, tiles, padded, width), half),
        pltpu.VMEM((n_exp, padded, width), half),
        pltpu.VMEM((n_exp, padded, width), half),
        pltpu.VMEM((n_exp, count, padded, width), half),
        pltpu.VMEM((n_exp, count, padded, width), half),
        pltpu.VMEM((comp, 2 * LANES), full),
        pltpu.VMEM((width // LANES, tiles * padded, LANES), full),
        pltpu.VMEM((mats, rows * group_exp, width), half),
        pltpu.VMEM((width // LANES, rows * group_exp, LANES), full),
        pltpu.VMEM((width // LANES, group_exp * padded, LANES), full),
        pltpu.VMEM((mats, rows * tiles, width), full),
        pltpu.VMEM((width // LANES, rows * tiles, LANES), full),
        pltpu.VMEM((tiles, padded, width), full),
        pltpu.VMEM((n_exp, padded, width), full),
        pltpu.VMEM((mats * group_exp, LANES), half),
        pltpu.VMEM((mats * tiles, LANES), half),
        pltpu.VMEM((group_exp, LANES, 2 * LANES), half),
        pltpu.VMEM((group_exp, 2 * LANES, LANES), half),
        *([sems((n_exp,))] * 6),
        *([sems((ITERS,))] * 4),
        *([sems((n_exp,))] * 8),
        *([pltpu.VMEM((n_exp, padded, width), half)] * 2),
    ]
    sky_out, residual = pl.pallas_call(
        functools.partial(kernel, n_grp, n_exp),
        out_shape=(
            jax.ShapeDtypeStruct((flat, width), full),
            jax.ShapeDtypeStruct((count, flat, width), full),
        ),
        in_specs=[pl.BlockSpec(memory_space=pltpu.HBM)] * len(operands),
        out_specs=(vmem, vmem),
        scratch_shapes=scratch,
        compiler_params=pltpu.CompilerParams(
            collective_id=0, has_side_effects=True, vmem_limit_bytes=64 * 2**20
        ),
    )(*operands)
    return sky_out.reshape(sky.shape), residual.reshape(observed.shape)


def solution(mesh):
    both = ("grp", "exp")
    in_specs = (
        P(both, None, None, None), P(both, None, None, None), P(both, None), P(both, None), P(both), P(), P(), P(),
    )
    out_specs = (P(both, None, None, None), P(both, None, None, None))
    body = functools.partial(shards, mesh.shape["grp"], mesh.shape["exp"])
    return jax.shard_map(body, mesh=mesh, in_specs=in_specs, out_specs=out_specs, check_vma=False)
```
